1024 devices in a mesh: hi: 32 (over z_hi, y), lo: 32 (over x, z_lo, core).
Axes of the slice: x: 8, y: 8, z: 8 (z_hi: 4, z_lo: 2; z = z_hi * 2 + z_lo), core: 2. Of those that a mesh axis runs over, the one named last changes fastest.
Arguments:
- state: bfloat16 [2, 268435456], P(None, ('hi', 'lo')), may hold values from -6 to 6
- gates: bfloat16 [4, 3, 2, 64, 64], replicated, may hold values from -0.5 to 0.5
- regroup: int32 [32], replicated, may hold values from 0 to 31, each once
Outputs:
- final_state: bfloat16 [2, 268435456], P(None, ('hi', 'lo'))
The draws below stay inside these ranges and needn't reach their ends.
Inputs may be any that keep to these rules, and one draw needn't show every extreme that they name: `regroup`: each value of 0 to 31 appears once.
All inputs are finite; a program needn't handle non-finite values.
Results may differ from the reference program's by a relative error of at most 0.02.
Values may be sent and summed in bfloat16 or wider, within the bound.
A program may use at most 32 MiB of HBM per device.

```python
import jax
import jax.numpy as jnp
from jax import lax

GQ = 6
G = 64
Q = 262144
LAYERS = 4
AMPS = 268435456
NLO = 32
N_HI = 32
N_LO = 32


def block_scale(stream_key, shape, shards, smallest, top_value):
    factor_of = 1.0
    for axis_at, parts in shards:
        draws = jax.random.uniform(jax.random.fold_in(jax.random.fold_in(stream_key, 6), axis_at), (parts,), jnp.float32, smallest / len(shards), top_value / len(shards))
        factor_of = factor_of * jnp.repeat(jnp.exp(draws), shape[axis_at] // parts).reshape((-1,) + (1,) * (len(shape) - 1 - axis_at))
    return factor_of


def scatter_about(stream_key, dims, spread, bound, pieces=(), kind=jnp.bfloat16):
    array = spread * jax.random.normal(stream_key, dims, jnp.float32)
    if pieces:
        array = array * block_scale(stream_key, dims, pieces, -0.22, 0.18)
    return jnp.clip(array, -bound, bound).astype(kind)


def setup_inputs(seed: int = 0) -> dict:
    splits = jax.random.split(jax.random.key(seed), 4)
    return {
        "state": scatter_about(splits[0], (2, AMPS), 1.0, 6.0, ((1, 1024),)),
        "gates": scatter_about(splits[1], (LAYERS, 3, 2, G, G), (2 * G) ** -0.5, 0.5),
        "regroup": jax.random.permutation(splits[2], NLO).astype(jnp.int32),
    }


def complex_block(gate):
    real_part = gate[0].astype(jnp.float32)
    imag_part = gate[1].astype(jnp.float32)
    upper = jnp.concatenate([real_part, -imag_part], axis=1)
    lower = jnp.concatenate([imag_part, real_part], axis=1)
    whole = jnp.concatenate([upper, lower], axis=0)
    return whole.reshape(2, G, 2, G)


def apply_gate(rows, matrix, block):
    inner = 2 ** (GQ * block)
    outer = Q // (inner * G)
    shaped = rows.reshape(2, rows.shape[1], outer, G, inner).astype(jnp.float32)
    result = jnp.einsum('qkpj,pnajb->qnakb', matrix, shaped)
    return result.astype(jnp.bfloat16).reshape(rows.shape)


def swap_hi(whole, hi_bit, local_bit):
    shaped = whole.reshape(2, N_HI // 2 ** (hi_bit + 1), 2, 2 ** hi_bit, N_LO, Q // 2 ** (local_bit + 1), 2, 2 ** local_bit)
    return jnp.swapaxes(shaped, 2, 6).reshape(whole.shape)


def reference(state, gates, regroup):
    whole = state.reshape(2, N_HI, N_LO, Q)
    hi_bits = int(N_HI).bit_length() - 1
    for layer in range(LAYERS):
        matrices = [complex_block(gates[layer, j]) for j in range(3)]

        def one_row(rows):
            for j in range(3):
                rows = apply_gate(rows, matrices[j], j)
            return rows

        moved = jnp.moveaxis(whole, 1, 0)
        moved = lax.map(one_row, moved)
        whole = jnp.moveaxis(moved, 0, 1)
        local_bit = 2 * GQ - 1 if layer % 2 == 0 else 3 * GQ - 1
        whole = swap_hi(whole, layer % hi_bits, local_bit)
        if layer == LAYERS // 2 - 1:
            shaped = whole.reshape(2, N_HI, N_LO, N_LO, Q // N_LO)
            taken = jnp.take(shaped, regroup.astype(jnp.int32), axis=3)
            whole = jnp.swapaxes(taken, 2, 3).reshape(2, N_HI, N_LO, Q)
    return whole.reshape(2, N_HI * N_LO * Q)
```

```python
import functools

import jax
import jax.numpy as jnp
from jax import lax
from jax.experimental import pallas as pl
from jax.experimental.pallas import tpu as pltpu
from jax.sharding import PartitionSpec as P

BF = jnp.bfloat16
F32 = jnp.float32
MESH = pl.DeviceIdType.MESH
CH = 4


def mm(a, b):
    return lax.dot_general(a, b, (((1,), (0,)), ((), ())), preferred_element_type=F32)


def mm_t(a, b):
    return lax.dot_general(a, b, (((1,), (1,)), ((), ())), preferred_element_type=F32)


def real_form(g_ref, layer, j):
    re = g_ref[layer, j, 0]
    im = g_ref[layer, j, 1]
    upper = jnp.concatenate([re, -im], axis=1)
    lower = jnp.concatenate([im, re], axis=1)
    return jnp.concatenate([upper, lower], axis=0)


def after(second, first):
    return mm(second, first).astype(BF)


def iotas(rows, cols):
    return (
        lax.broadcasted_iota(jnp.int32, (rows, cols), 0),
        lax.broadcasted_iota(jnp.int32, (rows, cols), 1),
    )


def middle_form(whole):
    i, j = iotas(128, 128)
    pick = jnp.where(j == (i // 32 % 2) * 64 + (i % 32) * 2 + i // 64, 1.0, 0.0).astype(BF)
    sorted_rows = mm(pick, whole).astype(BF)
    both = mm_t(sorted_rows, pick)
    upper = both[:64]
    lower = pltpu.roll(both[64:], 64, 1)
    return jnp.concatenate([upper, lower], axis=0).astype(BF)


def lane_form(whole):
    i, j = iotas(256, 128)
    spread = jnp.where(j == (i // 128) * 64 + i % 64, 1.0, 0.0).astype(BF)
    tall = mm(spread, whole).astype(BF)
    wide = mm_t(tall, spread)
    i, j = iotas(256, 256)
    return jnp.where(i // 64 % 2 == j // 64 % 2, wide, 0.0).astype(BF)


def middle_operand(re, im):
    return jnp.concatenate(
        [re.astype(BF), im.astype(BF), pltpu.roll(re, 64, 1).astype(BF), pltpu.roll(im, 64, 1).astype(BF)],
        axis=0,
    )


def middle_gate(weights, pairs):
    operand = jnp.concatenate([middle_operand(re, im) for re, im in pairs], axis=1)
    made = mm(weights, operand)
    low = lax.broadcasted_iota(jnp.int32, (32, 128), 1) < 64
    out = []
    for n in range(len(pairs)):
        part = made[:, 128 * n : 128 * (n + 1)]
        out.append(
            (
                jnp.where(low, part[0:32], part[64:96]).astype(BF),
                jnp.where(low, part[32:64], part[96:128]).astype(BF),
            )
        )
    return out


def kernel(n_lo, x_ref, g_ref, rg_ref, o_ref, *scratch):
    s1 = scratch[0:4]
    y1 = scratch[4:8]
    z1 = scratch[8:12]
    r1 = scratch[12:16]
    s2 = scratch[16:20]
    y2 = scratch[20:24]
    fa, fb, wc1, wb1, wb2, wa = scratch[24:30]
    ysend, yrecv, lsend, lrecv, psend, precv, own1, own2 = scratch[30:38]
    hi = lax.axis_index("hi")
    lo = lax.axis_index("lo")
    b0, b1, b2, b3 = hi % 2, hi // 2 % 2, hi // 4 % 2, hi // 8 % 2

    def near(d):
        return hi + (1 - 2 * b0) * (d % 2) + 2 * (1 - 2 * b1) * (d // 2)

    def far(d):
        return hi + 4 * (1 - 2 * b2) * (d % 2) + 8 * (1 - 2 * b3) * (d // 2)

    barrier = pltpu.get_barrier_semaphore()
    for d in range(1, 4):
        pl.semaphore_signal(barrier, inc=1, device_id={"hi": near(d), "lo": lo}, device_id_type=MESH)
        pl.semaphore_signal(barrier, inc=1, device_id={"hi": far(d), "lo": lo}, device_id_type=MESH)

    @pl.loop(1, n_lo)
    def _(j):
        pl.semaphore_signal(
            barrier, inc=1, device_id={"hi": hi, "lo": (lo + j) % n_lo}, device_id_type=MESH
        )

    c0 = after(real_form(g_ref, 1, 2), real_form(g_ref, 0, 2))

    @pl.loop(0, 16)
    def _(i):
        made = mm(c0, x_ref[:, pl.ds(pl.multiple_of(i * 256, 256), 256)])
        fa[pl.ds(pl.multiple_of(i * 256, 256), 128), :] = made[:, :128]
        fa[pl.ds(pl.multiple_of(i * 256 + 128, 128), 128), :] = made[:, 128:]

    def from_fa(c):
        return fa[pl.ds(c, 32, stride=128), :], fa[pl.ds(64 + c, 32, stride=128), :]

    wb0 = middle_form(real_form(g_ref, 0, 1))
    pl.semaphore_wait(barrier, 6 + n_lo - 1)

    def near_copy(ch, d):
        a = b0 + (1 - 2 * b0) * (d % 2)
        b = b1 + (1 - 2 * b1) * (d // 2)
        return pltpu.make_async_remote_copy(
            src_ref=s1[ch].at[b, a],
            dst_ref=y1[ch].at[b1, b0],
            send_sem=ysend.at[ch, d],
            recv_sem=yrecv.at[ch, d],
            device_id={"hi": near(d), "lo": lo},
            device_id_type=MESH,
        )

    def lo_copy(ch, j):
        to = (lo + j) % n_lo
        return pltpu.make_async_remote_copy(
            src_ref=z1[ch].at[to],
            dst_ref=r1[ch].at[lo],
            send_sem=lsend.at[ch, j],
            recv_sem=lrecv.at[ch, j],
            device_id={"hi": hi, "lo": to},
            device_id_type=MESH,
        )

    def far_copy(ch, d):
        a = b2 + (1 - 2 * b2) * (d % 2)
        b = b3 + (1 - 2 * b3) * (d // 2)
        return pltpu.make_async_remote_copy(
            src_ref=s2[ch].at[b, a],
            dst_ref=y2[ch].at[b3, b2],
            send_sem=psend.at[ch, d],
            recv_sem=precv.at[ch, d],
            device_id={"hi": far(d), "lo": lo},
            device_id_type=MESH,
        )

    def own_near(ch):
        return pltpu.make_async_copy(s1[ch].at[b1, b0], y1[ch].at[b1, b0], own1.at[ch])

    def own_far(ch):
        return pltpu.make_async_copy(s2[ch].at[b3, b2], y2[ch].at[b3, b2], own2.at[ch])

    for q12 in range(2):

        @pl.loop(0, 16)
        def _(u):
            c = u * 2 + q12
            done = middle_gate(wb0, [from_fa(c), from_fa(c + 32)])
            for b in range(2):
                for part in range(2):
                    for a in range(2):
                        s1[q12 * 2 + part][b, a, u] = done[b][part][16 * a : 16 * (a + 1)]

        for part in range(2):
            for d in (3, 2, 1):
                near_copy(q12 * 2 + part, d).start()
            own_near(q12 * 2 + part).start()

    wc1[...] = after(real_form(g_ref, 3, 2), real_form(g_ref, 2, 2))
    wb1[...] = middle_form(after(real_form(g_ref, 2, 1), real_form(g_ref, 1, 1)))
    wb2[...] = middle_form(real_form(g_ref, 3, 1))
    lane = after(real_form(g_ref, 1, 0), real_form(g_ref, 0, 0))
    lane2 = after(real_form(g_ref, 3, 0), real_form(g_ref, 2, 0))
    wa[...] = lane_form(after(lane2, lane))

    for ch in range(CH):
        for d in range(1, 4):
            near_copy(ch, d).wait_recv()
        own_near(ch).wait()

        @pl.loop(0, n_lo)
        def _(to):
            t = rg_ref[to]
            z1[ch][to, 0] = y1[ch][t // 16, 0, t % 16]
            z1[ch][to, 1] = y1[ch][t // 16, 1, t % 16]

        @pl.loop(1, n_lo)
        def _(j):
            lo_copy(ch, j).start()

    def spread_out(ch, ref, at, t):
        q12, part = ch // 2, ch % 2
        row = (part * 64 + t * 2 + q12) * 32
        for a in range(2):
            fb[pl.ds(pl.multiple_of(row + 16 * a, 16), 16), :] = ref[at, a].astype(F32)

    for ch in range(CH):

        @pl.loop(1, n_lo)
        def _(j):
            lo_copy(ch, j).wait_recv()

        spread_out(ch, z1[ch], lo, lo)

        @pl.loop(1, n_lo)
        def _(j):
            t = (lo + j) % n_lo
            spread_out(ch, r1[ch], t, t)

    @pl.loop(0, 16)
    def _(i):
        r = i * 2
        operand = jnp.concatenate(
            [
                fb[pl.ds(r, 128, stride=32), :].astype(BF),
                fb[pl.ds(r + 1, 128, stride=32), :].astype(BF),
            ],
            axis=1,
        )
        made = mm(wc1[...], operand)
        fa[pl.ds(pl.multiple_of(i * 256, 256), 128), :] = made[:, :128]
        fa[pl.ds(pl.multiple_of(i * 256 + 128, 128), 128), :] = made[:, 128:]

    for ch in range(CH):

        @pl.loop(0, 8)
        def _(v):
            c = ch * 8 + v
            done = middle_gate(wb1[...], [from_fa(c), from_fa(c + 32)])
            for b in range(2):
                for part in range(2):
                    for a in range(2):
                        s2[ch][b, a, v, part] = done[b][part][16 * a : 16 * (a + 1)]

        for d in (3, 2, 1):
            far_copy(ch, d).start()
        own_far(ch).start()

    for ch in range(CH):
        for d in range(1, 4):
            far_copy(ch, d).wait_recv()
        own_far(ch).wait()

        @pl.loop(0, 8)
        def _(v):
            pairs = []
            for b in range(2):
                pairs.append(
                    tuple(
                        jnp.concatenate(
                            [y2[ch][b, 0, v, part], y2[ch][b, 1, v, part]], axis=0
                        ).astype(F32)
                        for part in range(2)
                    )
                )
            done = middle_gate(wb2[...], pairs)
            operand = jnp.concatenate(
                [jnp.concatenate([re, im], axis=1) for re, im in done], axis=0
            )
            made = mm_t(operand, wa[...]).astype(BF)
            for b in range(2):
                row = pl.multiple_of((b * 32 + ch * 8 + v) * 32, 32)
                for part in range(2):
                    o_ref[part, pl.ds(row, 32), :] = made[
                        32 * b : 32 * (b + 1), 128 * part : 128 * (part + 1)
                    ]

    for ch in range(CH):
        for d in range(1, 4):
            near_copy(ch, d).wait_send()
            far_copy(ch, d).wait_send()

        @pl.loop(1, n_lo)
        def _(j):
            lo_copy(ch, j).wait_send()


def on_device(state, gates, regroup):
    n_lo = lax.axis_size("lo")
    vmem = pl.BlockSpec(memory_space=pltpu.VMEM)
    x = state.reshape(128, 4096)
    quarter = (2, 2, 16, 16, 128)
    by_lo = (n_lo, 2, 16, 128)
    scratch = (
        [pltpu.VMEM(quarter, BF)] * 8
        + [pltpu.VMEM(by_lo, BF)] * 8
        + [pltpu.VMEM((2, 2, 8, 2, 16, 128), BF)] * 8
        + [pltpu.VMEM((4096, 128), F32)] * 2
        + [pltpu.VMEM((128, 128), BF)] * 3
        + [pltpu.VMEM((256, 256), BF)]
        + [pltpu.SemaphoreType.DMA((CH, 4))] * 2
        + [pltpu.SemaphoreType.DMA((CH, n_lo))] * 2
        + [pltpu.SemaphoreType.DMA((CH, 4))] * 2
        + [pltpu.SemaphoreType.DMA((CH,))] * 2
    )
    out = pl.pallas_call(
        functools.partial(kernel, n_lo),
        out_shape=jax.ShapeDtypeStruct((2, 2048, 128), BF),
        in_specs=[vmem, vmem, pl.BlockSpec(memory_space=pltpu.SMEM)],
        out_specs=vmem,
        scratch_shapes=scratch,
        compiler_params=pltpu.CompilerParams(
            collective_id=0, has_side_effects=True, vmem_limit_bytes=40 * 1024 * 1024
        ),
        name="circuit",
    )(x, gates, regroup)
    return out.reshape(2, -1)


def solution(mesh):
    placed = (P(None, ("hi", "lo")), P(), P())
    return jax.shard_map(
        on_device, mesh=mesh, in_specs=placed, out_specs=P(None, ("hi", "lo")), check_vma=False
    )
```

```python
import functools

import jax
import jax.numpy as jnp
from jax import lax
from jax.experimental import pallas as pl
from jax.experimental.pallas import tpu as pltpu
from jax.sharding import PartitionSpec as P

BF = jnp.bfloat16
F32 = jnp.float32
MESH = pl.DeviceIdType.MESH
CH = 4
PA = 129
PB = 33


def mm(a, b):
    return lax.dot_general(a, b, (((1,), (0,)), ((), ())), preferred_element_type=F32)


def mm_t(a, b):
    return lax.dot_general(a, b, (((1,), (1,)), ((), ())), preferred_element_type=F32)


def real_form(g_ref, layer, j):
    re = g_ref[layer, j, 0]
    im = g_ref[layer, j, 1]
    upper = jnp.concatenate([re, -im], axis=1)
    lower = jnp.concatenate([im, re], axis=1)
    return jnp.concatenate([upper, lower], axis=0)


def after(second, first):
    return mm(second, first).astype(BF)


def iotas(rows, cols):
    return (
        lax.broadcasted_iota(jnp.int32, (rows, cols), 0),
        lax.broadcasted_iota(jnp.int32, (rows, cols), 1),
    )


def middle_form(whole, paired=False):
    i, j = iotas(128, 128)
    pick = jnp.where(j == (i // 32 % 2) * 64 + (i % 32) * 2 + i // 64, 1.0, 0.0).astype(BF)
    order = pick
    if paired:
        order = jnp.where(j == (i % 2) * 64 + i // 2 % 32 * 2 + i // 64, 1.0, 0.0).astype(BF)
    sorted_rows = mm(order, whole).astype(BF)
    both = mm_t(sorted_rows, pick)
    upper = both[:64]
    lower = pltpu.roll(both[64:], 64, 1)
    return jnp.concatenate([upper, lower], axis=0).astype(BF)


def lane_form(whole):
    i, j = iotas(256, 128)
    spread = jnp.where(j == (i // 128) * 64 + i % 64, 1.0, 0.0).astype(BF)
    tall = mm_t(spread, whole).astype(BF)
    wide = mm_t(tall, spread)
    i, j = iotas(256, 256)
    return jnp.where(i // 64 % 2 == j // 64 % 2, wide, 0.0).astype(BF)


def middle_operand(re, im):
    return jnp.concatenate(
        [re.astype(BF), im.astype(BF), pltpu.roll(re, 64, 1).astype(BF), pltpu.roll(im, 64, 1).astype(BF)],
        axis=0,
    )


def middle_gate(weights, pairs):
    operand = jnp.concatenate([middle_operand(re, im) for re, im in pairs], axis=1)
    made = mm(weights, operand)
    low = lax.broadcasted_iota(jnp.int32, (32, 128), 1) < 64
    out = []
    for n in range(len(pairs)):
        part = made[:, 128 * n : 128 * (n + 1)]
        out.append(
            (
                jnp.where(low, part[0:32], part[64:96]).astype(BF),
                jnp.where(low, part[32:64], part[96:128]).astype(BF),
            )
        )
    return out


def kernel(n_lo, x_ref, g_ref, rg_ref, o_ref, *scratch):
    s1 = scratch[0:4]
    y1 = scratch[4:8]
    z1 = scratch[8:12]
    r1 = scratch[12:16]
    s2 = scratch[16:20]
    y2 = scratch[20:24]
    fa, fb, wc1, wb1, wb2, wa = scratch[24:30]
    ysend, yrecv, lsend, lrecv, psend, precv = scratch[30:36]
    hi = lax.axis_index("hi")
    lo = lax.axis_index("lo")
    b0, b1, b2, b3 = hi % 2, hi // 2 % 2, hi // 4 % 2, hi // 8 % 2

    def near(d):
        return hi + (1 - 2 * b0) * (d % 2) + 2 * (1 - 2 * b1) * (d // 2)

    def far(d):
        return hi + 4 * (1 - 2 * b2) * (d % 2) + 8 * (1 - 2 * b3) * (d // 2)

    barrier = pltpu.get_barrier_semaphore()
    for d in range(1, 4):
        pl.semaphore_signal(barrier, inc=1, device_id={"hi": near(d), "lo": lo}, device_id_type=MESH)
        pl.semaphore_signal(barrier, inc=1, device_id={"hi": far(d), "lo": lo}, device_id_type=MESH)

    @pl.loop(1, n_lo)
    def _(j):
        pl.semaphore_signal(
            barrier, inc=1, device_id={"hi": hi, "lo": (lo + j) % n_lo}, device_id_type=MESH
        )

    c0 = after(real_form(g_ref, 1, 2), real_form(g_ref, 0, 2))

    @pl.loop(0, 16, unroll=4)
    def _(i):
        made = mm(c0, x_ref[:, pl.ds(pl.multiple_of(i * 256, 256), 256)])
        fa[pl.ds(2 * i * PA, 128), :] = made[:, :128]
        fa[pl.ds(2 * i * PA + PA, 128), :] = made[:, 128:]

    def from_fa(c):
        return fa[pl.ds(c, 32, stride=PA), :], fa[pl.ds(64 + c, 32, stride=PA), :]

    wb0 = middle_form(real_form(g_ref, 0, 1))
    pl.semaphore_wait(barrier, 6 + n_lo - 1)

    def near_copy(ch, d):
        a = b0 + (1 - 2 * b0) * (d % 2)
        b = b1 + (1 - 2 * b1) * (d // 2)
        return pltpu.make_async_remote_copy(
            src_ref=s1[ch].at[b, a],
            dst_ref=y1[ch].at[b1, b0],
            send_sem=ysend.at[ch, d],
            recv_sem=yrecv.at[ch, d],
            device_id={"hi": near(d), "lo": lo},
            device_id_type=MESH,
        )

    def lo_copy(ch, j):
        to = (lo + j) % n_lo
        return pltpu.make_async_remote_copy(
            src_ref=z1[ch].at[to],
            dst_ref=r1[ch].at[lo],
            send_sem=lsend.at[ch, j],
            recv_sem=lrecv.at[ch, j],
            device_id={"hi": hi, "lo": to},
            device_id_type=MESH,
        )

    def far_copy(ch, d):
        a = b2 + (1 - 2 * b2) * (d % 2)
        b = b3 + (1 - 2 * b3) * (d // 2)
        return pltpu.make_async_remote_copy(
            src_ref=s2[ch].at[b, a],
            dst_ref=y2[ch].at[b3, b2],
            send_sem=psend.at[ch, d],
            recv_sem=precv.at[ch, d],
            device_id={"hi": far(d), "lo": lo},
            device_id_type=MESH,
        )

    def own_near(ch):
        y1[ch][b1, b0] = s1[ch][b1, b0]

    def own_far(ch):
        y2[ch][b3, b2] = s2[ch][b3, b2]

    for q12 in range(2):

        @pl.loop(0, 16, unroll=4)
        def _(u):
            c = u * 2 + q12
            done = middle_gate(wb0, [from_fa(c), from_fa(c + 32)])
            for b in range(2):
                for part in range(2):
                    for a in range(2):
                        s1[q12 * 2 + part][b, a, u] = done[b][part][16 * a : 16 * (a + 1)]

        for part in range(2):
            for d in (3, 2, 1):
                near_copy(q12 * 2 + part, d).start()
            own_near(q12 * 2 + part)

    wc1[...] = after(real_form(g_ref, 3, 2), real_form(g_ref, 2, 2))
    wb1[...] = middle_form(after(real_form(g_ref, 2, 1), real_form(g_ref, 1, 1)))
    wb2[...] = middle_form(real_form(g_ref, 3, 1), paired=True)
    lane = after(real_form(g_ref, 1, 0), real_form(g_ref, 0, 0))
    lane2 = after(real_form(g_ref, 3, 0), real_form(g_ref, 2, 0))
    wa[...] = lane_form(after(lane2, lane))

    for ch in range(CH):
        for d in range(1, 4):
            near_copy(ch, d).wait_recv()

        @pl.loop(0, n_lo, unroll=4)
        def _(to):
            t = rg_ref[to]
            z1[ch][to, 0] = y1[ch][t // 16, 0, t % 16]
            z1[ch][to, 1] = y1[ch][t // 16, 1, t % 16]

        @pl.loop(1, n_lo)
        def _(j):
            lo_copy(ch, j).start()

    def spread_out(ch, ref, at, t):
        q12, part = ch // 2, ch % 2
        row = (part * 64 + t * 2 + q12) * PB
        for a in range(2):
            fb[pl.ds(row + 16 * a, 16), :] = ref[at, a].astype(F32)

    for ch in range(CH):

        @pl.loop(1, n_lo)
        def _(j):
            lo_copy(ch, j).wait_recv()

        spread_out(ch, z1[ch], lo, lo)

        @pl.loop(1, n_lo)
        def _(j):
            t = (lo + j) % n_lo
            spread_out(ch, r1[ch], t, t)

    @pl.loop(0, 16, unroll=4)
    def _(i):
        r = i * 2
        operand = jnp.concatenate(
            [
                fb[pl.ds(r, 128, stride=PB), :].astype(BF),
                fb[pl.ds(r + 1, 128, stride=PB), :].astype(BF),
            ],
            axis=1,
        )
        made = mm(wc1[...], operand)
        fa[pl.ds(2 * i * PA, 128), :] = made[:, :128]
        fa[pl.ds(2 * i * PA + PA, 128), :] = made[:, 128:]

    for ch in range(CH):

        @pl.loop(0, 8, unroll=4)
        def _(v):
            c = ch * 8 + v
            done = middle_gate(wb1[...], [from_fa(c), from_fa(c + 32)])
            for b in range(2):
                for part in range(2):
                    for a in range(2):
                        s2[ch][b, a, v, part] = done[b][part][16 * a : 16 * (a + 1)]

        for d in (3, 2, 1):
            far_copy(ch, d).start()
        own_far(ch)

    for ch in range(CH):
        for d in range(1, 4):
            far_copy(ch, d).wait_recv()

        @pl.loop(0, 2)
        def _(g):
            rows = []
            for k in range(4):
                for b in range(2):
                    for a in range(2):
                        rows.append(
                            jnp.concatenate(
                                [y2[ch][b, a, g * 4 + k, 0], y2[ch][b, a, g * 4 + k, 1]], axis=1
                            )
                        )
            made = mm(jnp.concatenate(rows, axis=0), wa[...])
            operand = jnp.concatenate(
                [
                    middle_operand(made[32 * n : 32 * n + 32, :128], made[32 * n : 32 * n + 32, 128:])
                    for n in range(8)
                ],
                axis=1,
            )
            whole = mm(wb2[...], operand)
            low = lax.broadcasted_iota(jnp.int32, (64, 128), 1) < 64
            for n in range(8):
                row = pl.multiple_of((n % 2 * 32 + ch * 8 + g * 4 + n // 2) * 64, 64)
                part = whole[:, 128 * n : 128 * (n + 1)]
                o_ref[pl.ds(row, 64), :] = jnp.where(low, part[:64], part[64:]).astype(BF)

    for ch in range(CH):
        for d in range(1, 4):
            near_copy(ch, d).wait_send()
            far_copy(ch, d).wait_send()

        @pl.loop(1, n_lo)
        def _(j):
            lo_copy(ch, j).wait_send()


def on_device(state, gates, regroup):
    n_lo = lax.axis_size("lo")
    vmem = pl.BlockSpec(memory_space=pltpu.VMEM)
    x = state.reshape(128, 4096)
    quarter = (2, 2, 16, 16, 128)
    by_lo = (n_lo, 2, 16, 128)
    scratch = (
        [pltpu.VMEM(quarter, BF)] * 8
        + [pltpu.VMEM(by_lo, BF)] * 8
        + [pltpu.VMEM((2, 2, 8, 2, 16, 128), BF)] * 8
        + [pltpu.VMEM((32 * PA, 128), F32), pltpu.VMEM((128 * PB, 128), F32)]
        + [pltpu.VMEM((128, 128), BF)] * 3
        + [pltpu.VMEM((256, 256), BF)]
        + [pltpu.SemaphoreType.DMA((CH, 4))] * 2
        + [pltpu.SemaphoreType.DMA((CH, n_lo))] * 2
        + [pltpu.SemaphoreType.DMA((CH, 4))] * 2
    )
    out = pl.pallas_call(
        functools.partial(kernel, n_lo),
        out_shape=jax.ShapeDtypeStruct((4096, 128), BF),
        in_specs=[vmem, vmem, pl.BlockSpec(memory_space=pltpu.SMEM)],
        out_specs=vmem,
        scratch_shapes=scratch,
        compiler_params=pltpu.CompilerParams(
            collective_id=0, has_side_effects=True, vmem_limit_bytes=40 * 1024 * 1024
        ),
        name="circuit",
    )(x, gates, regroup)
    return out.reshape(2048, 2, 128).transpose(1, 0, 2).reshape(2, -1)


def solution(mesh):
    placed = (P(None, ("hi", "lo")), P(), P())
    return jax.shard_map(
        on_device, mesh=mesh, in_specs=placed, out_specs=P(None, ("hi", "lo")), check_vma=False
    )
```

```python
import functools

import jax
import jax.numpy as jnp
from jax import lax
from jax.experimental import pallas as pl
from jax.experimental.pallas import tpu as pltpu
from jax.sharding import PartitionSpec as P

BF = jnp.bfloat16
F32 = jnp.float32
MESH = pl.DeviceIdType.MESH
CH = 4
SUB = 4
PA = 129
PB = 33
PC = 65


def mm(a, b):
    return lax.dot_general(a, b, (((1,), (0,)), ((), ())), preferred_element_type=F32)


def mm_t(a, b):
    return lax.dot_general(a, b, (((1,), (1,)), ((), ())), preferred_element_type=F32)


def real_form(g_ref, layer, j):
    re = g_ref[layer, j, 0]
    im = g_ref[layer, j, 1]
    upper = jnp.concatenate([re, -im], axis=1)
    lower = jnp.concatenate([im, re], axis=1)
    return jnp.concatenate([upper, lower], axis=0)


def after(second, first):
    return mm(second, first).astype(BF)


def iotas(rows, cols):
    return (
        lax.broadcasted_iota(jnp.int32, (rows, cols), 0),
        lax.broadcasted_iota(jnp.int32, (rows, cols), 1),
    )


def middle_form(whole, paired=False):
    i, j = iotas(128, 128)
    pick = jnp.where(j == (i // 32 % 2) * 64 + (i % 32) * 2 + i // 64, 1.0, 0.0).astype(BF)
    order = pick
    if paired:
        order = jnp.where(j == (i % 2) * 64 + i // 2 % 32 * 2 + i // 64, 1.0, 0.0).astype(BF)
    both = mm_t(mm(order, whole).astype(BF), pick)
    return jnp.concatenate([both[:64], pltpu.roll(both[64:], 64, 1)], axis=0).astype(BF)


def quarter_form(whole):
    i, j = iotas(128, 128)
    pick = jnp.where(j == (i // 64) * 64 + (i % 32) * 2 + i // 32 % 2, 1.0, 0.0).astype(BF)
    both = mm_t(mm(pick, whole).astype(BF), pick)
    rows = [both[:32]]
    for n in range(1, 4):
        rows.append(pltpu.roll(both[32 * n : 32 * n + 32], 128 - 32 * n, 1))
    return jnp.concatenate(rows, axis=0).astype(BF)


def half_form(whole):
    lower = pltpu.roll(whole[64:].astype(F32), 64, 1)
    return jnp.concatenate([whole[:64], lower.astype(BF)], axis=0)


def regrouped(i):
    return (i // 32 % 2) * 128 + (i // 128) * 64 + (i // 64 % 2) * 32 + i % 32


def lane_form(whole):
    i, j = iotas(256, 128)
    spread = jnp.where(j == (i // 128) * 64 + i % 64, 1.0, 0.0).astype(BF)
    wide = mm_t(mm_t(spread, whole).astype(BF), spread)
    i, j = iotas(256, 256)
    natural = jnp.where(i // 64 % 2 == j // 64 % 2, wide, 0.0).astype(BF)
    back = jnp.where(i == regrouped(j), 1.0, 0.0).astype(BF)
    return mm(back, natural).astype(BF)


def middle_operand(re, im):
    return jnp.concatenate(
        [re.astype(BF), im.astype(BF), pltpu.roll(re, 64, 1).astype(BF), pltpu.roll(im, 64, 1).astype(BF)],
        axis=0,
    )


def kernel(n_lo, x_ref, g_ref, rg_ref, o_ref, *scratch):
    s1 = scratch[0:4]
    y1 = scratch[4:8]
    z1 = scratch[8:12]
    r1 = scratch[12:16]
    s2 = scratch[16:24]
    y2 = scratch[24:32]
    m2 = scratch[32:40]
    fa, fb, wc1, wb1, wb2, wa, perm = scratch[40:47]
    ysend, yrecv, lsend, lrecv, psend, precv = scratch[47:53]
    hi = lax.axis_index("hi")
    lo = lax.axis_index("lo")
    b0, b1, b2, b3 = hi % 2, hi // 2 % 2, hi // 4 % 2, hi // 8 % 2
    y_peer = hi + 4 * (1 - 2 * b2)
    z_peer = hi + 8 * (1 - 2 * b3)

    def near(d):
        return hi + (1 - 2 * b0) * (d % 2) + 2 * (1 - 2 * b1) * (d // 2)

    barrier = pltpu.get_barrier_semaphore()
    for to in (near(1), near(2), near(3), y_peer, z_peer):
        pl.semaphore_signal(barrier, inc=1, device_id={"hi": to, "lo": lo}, device_id_type=MESH)

    @pl.loop(1, n_lo)
    def _(j):
        pl.semaphore_signal(
            barrier, inc=1, device_id={"hi": hi, "lo": (lo + j) % n_lo}, device_id_type=MESH
        )

    c0 = after(real_form(g_ref, 1, 2), real_form(g_ref, 0, 2))

    @pl.loop(0, 16, unroll=4)
    def _(i):
        made = mm(c0, x_ref[:, pl.ds(pl.multiple_of(i * 256, 256), 256)])
        fa[pl.ds(2 * i * PA, 128), :] = made[:, :128]
        fa[pl.ds(2 * i * PA + PA, 128), :] = made[:, 128:]

    wb0 = middle_form(real_form(g_ref, 0, 1))
    i, j = iotas(256, 256)
    perm[...] = jnp.where(j == regrouped(i), 1.0, 0.0).astype(BF)
    pl.semaphore_wait(barrier, 5 + n_lo - 1)

    def near_copy(ch, d):
        a = b0 + (1 - 2 * b0) * (d % 2)
        b = b1 + (1 - 2 * b1) * (d // 2)
        return pltpu.make_async_remote_copy(
            src_ref=s1[ch].at[b, a],
            dst_ref=y1[ch].at[b1, b0],
            send_sem=ysend.at[ch, d],
            recv_sem=yrecv.at[ch, d],
            device_id={"hi": near(d), "lo": lo},
            device_id_type=MESH,
        )

    def lo_copy(ch, j):
        to = (lo + j) % n_lo
        return pltpu.make_async_remote_copy(
            src_ref=z1[ch].at[to],
            dst_ref=r1[ch].at[lo],
            send_sem=lsend.at[ch, j],
            recv_sem=lrecv.at[ch, j],
            device_id={"hi": hi, "lo": to},
            device_id_type=MESH,
        )

    def far_copy(k, kind):
        src, dst, to = (
            (m2[k], y2[k].at[1 - b3, b2], y_peer),
            (s2[k].at[b3, 1 - b2], y2[k].at[b3, b2], y_peer),
            (s2[k].at[1 - b3, b2], y2[k].at[b3, b2], z_peer),
            (s2[k].at[1 - b3, 1 - b2], m2[k], z_peer),
        )[kind]
        return pltpu.make_async_remote_copy(
            src_ref=src,
            dst_ref=dst,
            send_sem=psend.at[k, kind],
            recv_sem=precv.at[k, kind],
            device_id={"hi": to, "lo": lo},
            device_id_type=MESH,
        )

    def send_near(ch):
        for d in (3, 2, 1):
            near_copy(ch, d).start()
        y1[ch][b1, b0] = s1[ch][b1, b0]

    low = lax.broadcasted_iota(jnp.int32, (32, 128), 1) < 64
    for q12 in range(2):

        @pl.loop(0, 4)
        def _(g):
            parts = []
            for k in range(4):
                for b in range(2):
                    c = b * 32 + (g * 4 + k) * 2 + q12
                    parts.append(
                        middle_operand(
                            fa[pl.ds(c, 32, stride=PA), :], fa[pl.ds(64 + c, 32, stride=PA), :]
                        )
                    )
            made = mm(wb0, jnp.concatenate(parts, axis=1))
            rows = []
            for n in range(8):
                part = made[:, 128 * n : 128 * (n + 1)]
                re = jnp.where(low, part[0:32], part[64:96]).astype(BF)
                im = jnp.where(low, part[32:64], part[96:128]).astype(BF)
                rows.append(jnp.concatenate([re, im], axis=1))
            moved = mm(jnp.concatenate(rows, axis=0), perm[...]).astype(BF)
            for n in range(8):
                for e in range(2):
                    for a in range(2):
                        s1[e * 2 + q12][n % 2, a, g * 4 + n // 2] = moved[
                            32 * n + 16 * a : 32 * n + 16 * a + 16, 128 * e : 128 * (e + 1)
                        ]

        send_near(q12)
    send_near(2)
    send_near(3)

    wc1[...] = half_form(after(real_form(g_ref, 3, 2), real_form(g_ref, 2, 2)))
    wb1[...] = quarter_form(after(real_form(g_ref, 2, 1), real_form(g_ref, 1, 1)))
    wb2[...] = middle_form(real_form(g_ref, 3, 1), paired=True)
    lane = after(real_form(g_ref, 1, 0), real_form(g_ref, 0, 0))
    lane2 = after(real_form(g_ref, 3, 0), real_form(g_ref, 2, 0))
    wa[...] = lane_form(after(lane2, lane))

    def pass_to_lo(ch):
        for d in range(1, 4):
            near_copy(ch, d).wait_recv()

        @pl.loop(0, n_lo, unroll=4)
        def _(to):
            t = rg_ref[to]
            z1[ch][to, 0] = y1[ch][t // 16, 0, t % 16]
            z1[ch][to, 1] = y1[ch][t // 16, 1, t % 16]

        @pl.loop(1, n_lo)
        def _(j):
            lo_copy(ch, j).start()

    def spread_out(ch, ref, t):
        for a in range(2):
            fb[pl.ds((t * 2 + ch % 2) * PB + 16 * a, 16), :] = ref[t, a].astype(F32)

    def take_from_lo(ch):
        spread_out(ch, z1[ch], lo)

        @pl.loop(1, n_lo)
        def _(j):
            lo_copy(ch, j).wait_recv()

        @pl.loop(1, n_lo)
        def _(j):
            spread_out(ch, r1[ch], (lo + j) % n_lo)

    def top_gate():
        left = lax.broadcasted_iota(jnp.int32, (64, 128), 1) < 64

        @pl.loop(0, 8)
        def _(g):
            parts = []
            for k in range(4):
                x = fb[pl.ds(g * 4 + k, 64, stride=PB), :]
                parts.append(
                    jnp.concatenate([x.astype(BF), pltpu.roll(x, 64, 1).astype(BF)], axis=0)
                )
            made = mm(wc1[...], jnp.concatenate(parts, axis=1))
            for k in range(4):
                part = made[:, 128 * k : 128 * (k + 1)]
                fa[pl.ds((g * 4 + k) * PC, 64), :] = jnp.where(left, part[:64], part[64:])

    quarter = lax.broadcasted_iota(jnp.int32, (32, 128), 1) // 32

    def middle_and_send(e, n_sub):
        at = e * SUB + n_sub

        @pl.loop(0, 2)
        def _(g):
            parts = []
            for k in range(4):
                for b in range(2):
                    x = fa[pl.ds(b * 32 + n_sub * 8 + g * 4 + k, 32, stride=PC), :]
                    parts.append(
                        jnp.concatenate(
                            [x.astype(BF)]
                            + [pltpu.roll(x, 128 - 32 * m, 1).astype(BF) for m in range(1, 4)],
                            axis=0,
                        )
                    )
            made = mm(wb1[...], jnp.concatenate(parts, axis=1))
            for n in range(8):
                part = made[:, 128 * n : 128 * (n + 1)]
                first = jnp.where(quarter == 0, part[0:32], part[32:64])
                second = jnp.where(quarter == 2, part[64:96], part[96:128])
                done = jnp.where(quarter < 2, first, second).astype(BF)
                for a in range(2):
                    s2[at][n % 2, a, g * 4 + n // 2] = done[16 * a : 16 * (a + 1)]

        for kind in (3, 1, 2):
            far_copy(at, kind).start()
        y2[at][b3, b2] = s2[at][b3, b2]

    def pass_on(at):
        far_copy(at, 3).wait_recv()
        far_copy(at, 0).start()

    pass_to_lo(0)
    pass_to_lo(1)
    take_from_lo(0)
    take_from_lo(1)
    top_gate()
    for n_sub in range(SUB):
        middle_and_send(0, n_sub)
    pass_to_lo(2)
    pass_on(0)
    pass_on(1)
    pass_to_lo(3)
    pass_on(2)
    pass_on(3)
    take_from_lo(2)
    take_from_lo(3)
    top_gate()
    for n_sub in range(SUB):
        middle_and_send(1, n_sub)
    for n_sub in range(SUB):
        pass_on(SUB + n_sub)

    for ch in range(SUB):
        for e in range(2):
            for kind in range(3):
                far_copy(e * SUB + ch, kind).wait_recv()

        @pl.loop(0, 2)
        def _(g):
            rows = []
            for k in range(4):
                for b in range(2):
                    for a in range(2):
                        rows.append(
                            jnp.concatenate(
                                [y2[ch][b, a, g * 4 + k], y2[SUB + ch][b, a, g * 4 + k]], axis=1
                            )
                        )
            made = mm(jnp.concatenate(rows, axis=0), wa[...])
            operand = jnp.concatenate(
                [
                    middle_operand(made[32 * n : 32 * n + 32, :128], made[32 * n : 32 * n + 32, 128:])
                    for n in range(8)
                ],
                axis=1,
            )
            whole = mm(wb2[...], operand)
            left = lax.broadcasted_iota(jnp.int32, (64, 128), 1) < 64
            for n in range(8):
                row = pl.multiple_of((n % 2 * 32 + ch * 8 + g * 4 + n // 2) * 64, 64)
                part = whole[:, 128 * n : 128 * (n + 1)]
                o_ref[pl.ds(row, 64), :] = jnp.where(left, part[:64], part[64:]).astype(BF)

    for ch in range(CH):
        for d in range(1, 4):
            near_copy(ch, d).wait_send()

        @pl.loop(1, n_lo)
        def _(j):
            lo_copy(ch, j).wait_send()

    for at in range(2 * SUB):
        for kind in range(4):
            far_copy(at, kind).wait_send()


def on_device(state, gates, regroup):
    n_lo = lax.axis_size("lo")
    vmem = pl.BlockSpec(memory_space=pltpu.VMEM)
    x = state.reshape(128, 4096)
    quarter = (2, 2, 16, 16, 128)
    by_lo = (n_lo, 2, 16, 128)
    scratch = (
        [pltpu.VMEM(quarter, BF)] * 8
        + [pltpu.VMEM(by_lo, BF)] * 8
        + [pltpu.VMEM((2, 2, 8, 16, 128), BF)] * 16
        + [pltpu.VMEM((8, 16, 128), BF)] * 8
        + [pltpu.VMEM((32 * PA, 128), F32), pltpu.VMEM((64 * PB, 128), F32)]
        + [pltpu.VMEM((128, 128), BF)] * 3
        + [pltpu.VMEM((256, 256), BF)] * 2
        + [pltpu.SemaphoreType.DMA((CH, 4))] * 2
        + [pltpu.SemaphoreType.DMA((CH, n_lo))] * 2
        + [pltpu.SemaphoreType.DMA((2 * SUB, 4))] * 2
    )
    out = pl.pallas_call(
        functools.partial(kernel, n_lo),
        out_shape=jax.ShapeDtypeStruct((4096, 128), BF),
        in_specs=[vmem, vmem, pl.BlockSpec(memory_space=pltpu.SMEM)],
        out_specs=vmem,
        scratch_shapes=scratch,
        compiler_params=pltpu.CompilerParams(
            collective_id=0, has_side_effects=True, vmem_limit_bytes=40 * 1024 * 1024
        ),
        name="circuit",
    )(x, gates, regroup)
    return out.reshape(2048, 2, 128).transpose(1, 0, 2).reshape(2, -1)


def solution(mesh):
    placed = (P(None, ("hi", "lo")), P(), P())
    return jax.shard_map(
        on_device, mesh=mesh, in_specs=placed, out_specs=P(None, ("hi", "lo")), check_vma=False
    )
```

```python
import functools

import jax
import jax.numpy as jnp
from jax import lax
from jax.experimental import pallas as pl
from jax.experimental.pallas import tpu as pltpu
from jax.sharding import PartitionSpec as P

BF = jnp.bfloat16
F32 = jnp.float32
MESH = pl.DeviceIdType.MESH
CH = 4
SUB = 4
PA = 129
PB = 33
PC = 65


def mm(a, b):
    return lax.dot_general(a, b, (((1,), (0,)), ((), ())), preferred_element_type=F32)


def mm_t(a, b):
    return lax.dot_general(a, b, (((1,), (1,)), ((), ())), preferred_element_type=F32)


def real_form(g_ref, layer, j):
    re = g_ref[layer, j, 0]
    im = g_ref[layer, j, 1]
    upper = jnp.concatenate([re, -im], axis=1)
    lower = jnp.concatenate([im, re], axis=1)
    return jnp.concatenate([upper, lower], axis=0)


def after(second, first):
    return mm(second, first).astype(BF)


def iotas(rows, cols):
    return (
        lax.broadcasted_iota(jnp.int32, (rows, cols), 0),
        lax.broadcasted_iota(jnp.int32, (rows, cols), 1),
    )


def middle_form(whole, paired=False):
    i, j = iotas(128, 128)
    pick = jnp.where(j == (i // 32 % 2) * 64 + (i % 32) * 2 + i // 64, 1.0, 0.0).astype(BF)
    order = pick
    if paired:
        order = jnp.where(j == (i % 2) * 64 + i // 2 % 32 * 2 + i // 64, 1.0, 0.0).astype(BF)
    both = mm_t(mm(order, whole).astype(BF), pick)
    return jnp.concatenate([both[:64], pltpu.roll(both[64:], 64, 1)], axis=0).astype(BF)


def quarter_form(whole):
    i, j = iotas(128, 128)
    pick = jnp.where(j == (i // 64) * 64 + (i % 32) * 2 + i // 32 % 2, 1.0, 0.0).astype(BF)
    both = mm_t(mm(pick, whole).astype(BF), pick)
    rows = [both[:32]]
    for n in range(1, 4):
        rows.append(pltpu.roll(both[32 * n : 32 * n + 32], 128 - 32 * n, 1))
    return jnp.concatenate(rows, axis=0).astype(BF)


def half_form(whole):
    lower = pltpu.roll(whole[64:].astype(F32), 64, 1)
    return jnp.concatenate([whole[:64], lower.astype(BF)], axis=0)


def regrouped(i):
    return (i // 32 % 2) * 128 + (i // 128) * 64 + (i // 64 % 2) * 32 + i % 32


def lane_form(whole):
    i, j = iotas(256, 128)
    spread = jnp.where(j == (i // 128) * 64 + i % 64, 1.0, 0.0).astype(BF)
    wide = mm_t(mm_t(spread, whole).astype(BF), spread)
    i, j = iotas(256, 256)
    natural = jnp.where(i // 64 % 2 == j // 64 % 2, wide, 0.0).astype(BF)
    back = jnp.where(i == regrouped(j), 1.0, 0.0).astype(BF)
    return mm(back, natural).astype(BF)


def middle_operand(re, im):
    return jnp.concatenate(
        [re.astype(BF), im.astype(BF), pltpu.roll(re, 64, 1).astype(BF), pltpu.roll(im, 64, 1).astype(BF)],
        axis=0,
    )


def kernel(n_lo, x_ref, g_ref, rg_ref, o_ref, *scratch):
    s1 = scratch[0:4]
    y1 = scratch[4:8]
    z1 = scratch[8:12]
    r1 = scratch[12:16]
    s2 = scratch[16:24]
    y2 = scratch[24:32]
    fa, fb, wc1, wb1, wb2, wa, perm = scratch[32:39]
    ysend, yrecv, lsend, lrecv, psend, precv = scratch[39:45]
    hi = lax.axis_index("hi")
    lo = lax.axis_index("lo")
    b0, b1, b2, b3 = hi % 2, hi // 2 % 2, hi // 4 % 2, hi // 8 % 2

    def near(d):
        return hi + (1 - 2 * b0) * (d % 2) + 2 * (1 - 2 * b1) * (d // 2)

    def far(d):
        return hi + 4 * (1 - 2 * b2) * (d % 2) + 8 * (1 - 2 * b3) * (d // 2)

    barrier = pltpu.get_barrier_semaphore()
    for to in (near(1), near(2), near(3), far(1), far(2), far(3)):
        pl.semaphore_signal(barrier, inc=1, device_id={"hi": to, "lo": lo}, device_id_type=MESH)

    @pl.loop(1, n_lo)
    def _(j):
        pl.semaphore_signal(
            barrier, inc=1, device_id={"hi": hi, "lo": (lo + j) % n_lo}, device_id_type=MESH
        )

    c0 = after(real_form(g_ref, 1, 2), real_form(g_ref, 0, 2))

    @pl.loop(0, 16, unroll=4)
    def _(i):
        made = mm(c0, x_ref[:, pl.ds(pl.multiple_of(i * 256, 256), 256)])
        fa[pl.ds(2 * i * PA, 128), :] = made[:, :128]
        fa[pl.ds(2 * i * PA + PA, 128), :] = made[:, 128:]

    wb0 = middle_form(real_form(g_ref, 0, 1))
    i, j = iotas(256, 256)
    perm[...] = jnp.where(j == regrouped(i), 1.0, 0.0).astype(BF)
    pl.semaphore_wait(barrier, 6 + n_lo - 1)

    def near_copy(ch, d):
        a = b0 + (1 - 2 * b0) * (d % 2)
        b = b1 + (1 - 2 * b1) * (d // 2)
        return pltpu.make_async_remote_copy(
            src_ref=s1[ch].at[b, a],
            dst_ref=y1[ch].at[b1, b0],
            send_sem=ysend.at[ch, d],
            recv_sem=yrecv.at[ch, d],
            device_id={"hi": near(d), "lo": lo},
            device_id_type=MESH,
        )

    def lo_copy(ch, j):
        to = (lo + j) % n_lo
        return pltpu.make_async_remote_copy(
            src_ref=z1[ch].at[to],
            dst_ref=r1[ch].at[lo],
            send_sem=lsend.at[ch, j],
            recv_sem=lrecv.at[ch, j],
            device_id={"hi": hi, "lo": to},
            device_id_type=MESH,
        )

    def far_copy(k, kind):
        a = b2 + (1 - 2 * b2) * (kind % 2)
        b = b3 + (1 - 2 * b3) * (kind // 2)
        src, dst, to = s2[k].at[b, a], y2[k].at[b3, b2], far(kind)
        return pltpu.make_async_remote_copy(
            src_ref=src,
            dst_ref=dst,
            send_sem=psend.at[k, kind],
            recv_sem=precv.at[k, kind],
            device_id={"hi": to, "lo": lo},
            device_id_type=MESH,
        )

    def send_near(ch):
        for d in (3, 2, 1):
            near_copy(ch, d).start()
        y1[ch][b1, b0] = s1[ch][b1, b0]

    low = lax.broadcasted_iota(jnp.int32, (32, 128), 1) < 64
    for q12 in range(2):

        @pl.loop(0, 4)
        def _(g):
            parts = []
            for k in range(4):
                for b in range(2):
                    c = b * 32 + (g * 4 + k) * 2 + q12
                    parts.append(
                        middle_operand(
                            fa[pl.ds(c, 32, stride=PA), :], fa[pl.ds(64 + c, 32, stride=PA), :]
                        )
                    )
            made = mm(wb0, jnp.concatenate(parts, axis=1))
            rows = []
            for n in range(8):
                part = made[:, 128 * n : 128 * (n + 1)]
                re = jnp.where(low, part[0:32], part[64:96]).astype(BF)
                im = jnp.where(low, part[32:64], part[96:128]).astype(BF)
                rows.append(jnp.concatenate([re, im], axis=1))
            moved = mm(jnp.concatenate(rows, axis=0), perm[...]).astype(BF)
            for n in range(8):
                for e in range(2):
                    for a in range(2):
                        s1[e * 2 + q12][n % 2, a, g * 4 + n // 2] = moved[
                            32 * n + 16 * a : 32 * n + 16 * a + 16, 128 * e : 128 * (e + 1)
                        ]

        send_near(q12)
    send_near(2)
    send_near(3)

    wc1[...] = half_form(after(real_form(g_ref, 3, 2), real_form(g_ref, 2, 2)))
    wb1[...] = quarter_form(after(real_form(g_ref, 2, 1), real_form(g_ref, 1, 1)))
    wb2[...] = middle_form(real_form(g_ref, 3, 1), paired=True)
    lane = after(real_form(g_ref, 1, 0), real_form(g_ref, 0, 0))
    lane2 = after(real_form(g_ref, 3, 0), real_form(g_ref, 2, 0))
    wa[...] = lane_form(after(lane2, lane))

    def pass_to_lo(ch):
        for d in range(1, 4):
            near_copy(ch, d).wait_recv()

        @pl.loop(0, n_lo, unroll=4)
        def _(to):
            t = rg_ref[to]
            z1[ch][to, 0] = y1[ch][t // 16, 0, t % 16]
            z1[ch][to, 1] = y1[ch][t // 16, 1, t % 16]

        @pl.loop(1, n_lo)
        def _(j):
            lo_copy(ch, j).start()

    def spread_out(ch, ref, t):
        for a in range(2):
            fb[pl.ds((t * 2 + ch % 2) * PB + 16 * a, 16), :] = ref[t, a].astype(F32)

    def take_from_lo(ch):
        spread_out(ch, z1[ch], lo)

        @pl.loop(1, n_lo)
        def _(j):
            lo_copy(ch, j).wait_recv()

        @pl.loop(1, n_lo)
        def _(j):
            spread_out(ch, r1[ch], (lo + j) % n_lo)

    def top_gate():
        left = lax.broadcasted_iota(jnp.int32, (64, 128), 1) < 64

        @pl.loop(0, 8)
        def _(g):
            parts = []
            for k in range(4):
                x = fb[pl.ds(g * 4 + k, 64, stride=PB), :]
                parts.append(
                    jnp.concatenate([x.astype(BF), pltpu.roll(x, 64, 1).astype(BF)], axis=0)
                )
            made = mm(wc1[...], jnp.concatenate(parts, axis=1))
            for k in range(4):
                part = made[:, 128 * k : 128 * (k + 1)]
                fa[pl.ds((g * 4 + k) * PC, 64), :] = jnp.where(left, part[:64], part[64:])

    quarter = lax.broadcasted_iota(jnp.int32, (32, 128), 1) // 32

    def middle_and_send(e, n_sub):
        at = e * SUB + n_sub

        @pl.loop(0, 2)
        def _(g):
            parts = []
            for k in range(4):
                for b in range(2):
                    x = fa[pl.ds(b * 32 + n_sub * 8 + g * 4 + k, 32, stride=PC), :]
                    parts.append(
                        jnp.concatenate(
                            [x.astype(BF)]
                            + [pltpu.roll(x, 128 - 32 * m, 1).astype(BF) for m in range(1, 4)],
                            axis=0,
                        )
                    )
            made = mm(wb1[...], jnp.concatenate(parts, axis=1))
            for n in range(8):
                part = made[:, 128 * n : 128 * (n + 1)]
                first = jnp.where(quarter == 0, part[0:32], part[32:64])
                second = jnp.where(quarter == 2, part[64:96], part[96:128])
                done = jnp.where(quarter < 2, first, second).astype(BF)
                for a in range(2):
                    s2[at][n % 2, a, g * 4 + n // 2] = done[16 * a : 16 * (a + 1)]

        for kind in (3, 2, 1):
            far_copy(at, kind).start()
        y2[at][b3, b2] = s2[at][b3, b2]

    for ch in range(CH):
        pass_to_lo(ch)
    take_from_lo(0)
    take_from_lo(1)
    top_gate()
    for n_sub in range(SUB):
        middle_and_send(0, n_sub)
    take_from_lo(2)
    take_from_lo(3)
    top_gate()
    for n_sub in range(SUB):
        middle_and_send(1, n_sub)
    for ch in range(SUB):
        for e in range(2):
            for kind in range(1, 4):
                far_copy(e * SUB + ch, kind).wait_recv()

        @pl.loop(0, 2)
        def _(g):
            rows = []
            for k in range(4):
                for b in range(2):
                    for a in range(2):
                        rows.append(
                            jnp.concatenate(
                                [y2[ch][b, a, g * 4 + k], y2[SUB + ch][b, a, g * 4 + k]], axis=1
                            )
                        )
            made = mm(jnp.concatenate(rows, axis=0), wa[...])
            operand = jnp.concatenate(
                [
                    middle_operand(made[32 * n : 32 * n + 32, :128], made[32 * n : 32 * n + 32, 128:])
                    for n in range(8)
                ],
                axis=1,
            )
            whole = mm(wb2[...], operand)
            left = lax.broadcasted_iota(jnp.int32, (64, 128), 1) < 64
            for n in range(8):
                row = pl.multiple_of((n % 2 * 32 + ch * 8 + g * 4 + n // 2) * 64, 64)
                part = whole[:, 128 * n : 128 * (n + 1)]
                o_ref[pl.ds(row, 64), :] = jnp.where(left, part[:64], part[64:]).astype(BF)

    for ch in range(CH):
        for d in range(1, 4):
            near_copy(ch, d).wait_send()

        @pl.loop(1, n_lo)
        def _(j):
            lo_copy(ch, j).wait_send()

    for at in range(2 * SUB):
        for kind in range(1, 4):
            far_copy(at, kind).wait_send()


def on_device(state, gates, regroup):
    n_lo = lax.axis_size("lo")
    vmem = pl.BlockSpec(memory_space=pltpu.VMEM)
    x = state.reshape(128, 4096)
    quarter = (2, 2, 16, 16, 128)
    by_lo = (n_lo, 2, 16, 128)
    scratch = (
        [pltpu.VMEM(quarter, BF)] * 8
        + [pltpu.VMEM(by_lo, BF)] * 8
        + [pltpu.VMEM((2, 2, 8, 16, 128), BF)] * 16
        + [pltpu.VMEM((32 * PA, 128), F32), pltpu.VMEM((64 * PB, 128), F32)]
        + [pltpu.VMEM((128, 128), BF)] * 3
        + [pltpu.VMEM((256, 256), BF)] * 2
        + [pltpu.SemaphoreType.DMA((CH, 4))] * 2
        + [pltpu.SemaphoreType.DMA((CH, n_lo))] * 2
        + [pltpu.SemaphoreType.DMA((2 * SUB, 4))] * 2
    )
    out = pl.pallas_call(
        functools.partial(kernel, n_lo),
        out_shape=jax.ShapeDtypeStruct((4096, 128), BF),
        in_specs=[vmem, vmem, pl.BlockSpec(memory_space=pltpu.SMEM)],
        out_specs=vmem,
        scratch_shapes=scratch,
        compiler_params=pltpu.CompilerParams(
            collective_id=0, has_side_effects=True, vmem_limit_bytes=40 * 1024 * 1024
        ),
        name="circuit",
    )(x, gates, regroup)
    return out.reshape(2048, 2, 128).transpose(1, 0, 2).reshape(2, -1)


def solution(mesh):
    placed = (P(None, ("hi", "lo")), P(), P())
    return jax.shard_map(
        on_device, mesh=mesh, in_specs=placed, out_specs=P(None, ("hi", "lo")), check_vma=False
    )
```

```python
import functools

import jax
import jax.numpy as jnp
from jax import lax
from jax.experimental import pallas as pl
from jax.experimental.pallas import tpu as pltpu
from jax.sharding import PartitionSpec as P

BF = jnp.bfloat16
F32 = jnp.float32
MESH = pl.DeviceIdType.MESH
CH = 3
SUB = 4
PA = 129
PB = 33
PC = 65


def mm(a, b):
    return lax.dot_general(a, b, (((1,), (0,)), ((), ())), preferred_element_type=F32)


def mm_t(a, b):
    return lax.dot_general(a, b, (((1,), (1,)), ((), ())), preferred_element_type=F32)


def real_form(g_ref, layer, j):
    re = g_ref[layer, j, 0]
    im = g_ref[layer, j, 1]
    upper = jnp.concatenate([re, -im], axis=1)
    lower = jnp.concatenate([im, re], axis=1)
    return jnp.concatenate([upper, lower], axis=0)


def after(second, first):
    return mm(second, first).astype(BF)


def iotas(rows, cols):
    return (
        lax.broadcasted_iota(jnp.int32, (rows, cols), 0),
        lax.broadcasted_iota(jnp.int32, (rows, cols), 1),
    )


def middle_form(whole, paired=False):
    i, j = iotas(128, 128)
    pick = jnp.where(j == (i // 32 % 2) * 64 + (i % 32) * 2 + i // 64, 1.0, 0.0).astype(BF)
    order = pick
    if paired:
        order = jnp.where(j == (i % 2) * 64 + i // 2 % 32 * 2 + i // 64, 1.0, 0.0).astype(BF)
    both = mm_t(mm(order, whole).astype(BF), pick)
    return jnp.concatenate([both[:64], pltpu.roll(both[64:], 64, 1)], axis=0).astype(BF)


def quarter_form(whole):
    i, j = iotas(128, 128)
    pick = jnp.where(j == (i // 64) * 64 + (i % 32) * 2 + i // 32 % 2, 1.0, 0.0).astype(BF)
    both = mm_t(mm(pick, whole).astype(BF), pick)
    rows = [both[:32]]
    for n in range(1, 4):
        rows.append(pltpu.roll(both[32 * n : 32 * n + 32], 128 - 32 * n, 1))
    return jnp.concatenate(rows, axis=0).astype(BF)


def half_form(whole):
    lower = pltpu.roll(whole[64:].astype(F32), 64, 1)
    return jnp.concatenate([whole[:64], lower.astype(BF)], axis=0)


def regrouped(i):
    return (i // 32 % 2) * 128 + (i // 128) * 64 + (i // 64 % 2) * 32 + i % 32


def lane_form(whole):
    i, j = iotas(256, 128)
    spread = jnp.where(j == (i // 128) * 64 + i % 64, 1.0, 0.0).astype(BF)
    wide = mm_t(mm_t(spread, whole).astype(BF), spread)
    i, j = iotas(256, 256)
    natural = jnp.where(i // 64 % 2 == j // 64 % 2, wide, 0.0).astype(BF)
    back = jnp.where(i == regrouped(j), 1.0, 0.0).astype(BF)
    return mm(back, natural).astype(BF)


def middle_operand(re, im):
    return jnp.concatenate(
        [re.astype(BF), im.astype(BF), pltpu.roll(re, 64, 1).astype(BF), pltpu.roll(im, 64, 1).astype(BF)],
        axis=0,
    )


def kernel(n_lo, x_ref, g_ref, rg_ref, o_ref, *scratch):
    s1 = scratch[0:3]
    y1 = scratch[3:6]
    z1 = scratch[6:9]
    r1 = scratch[9:12]
    s2 = scratch[12:20]
    y2 = scratch[20:28]
    fa, fb, fx, wc1, wb1, wb2, wa, perm = scratch[28:36]
    ysend, yrecv, lsend, lrecv, psend, precv = scratch[36:42]
    hi = lax.axis_index("hi")
    lo = lax.axis_index("lo")
    b0, b1, b2, b3 = hi % 2, hi // 2 % 2, hi // 4 % 2, hi // 8 % 2

    def near(d):
        return hi + (1 - 2 * b0) * (d % 2) + 2 * (1 - 2 * b1) * (d // 2)

    def far(d):
        return hi + 4 * (1 - 2 * b2) * (d % 2) + 8 * (1 - 2 * b3) * (d // 2)

    barrier = pltpu.get_barrier_semaphore()
    for to in (near(1), near(2), near(3), far(1), far(2), far(3)):
        pl.semaphore_signal(barrier, inc=1, device_id={"hi": to, "lo": lo}, device_id_type=MESH)

    @pl.loop(1, n_lo)
    def _(j):
        pl.semaphore_signal(
            barrier, inc=1, device_id={"hi": hi, "lo": (lo + j) % n_lo}, device_id_type=MESH
        )

    c0 = after(real_form(g_ref, 1, 2), real_form(g_ref, 0, 2))

    @pl.loop(0, 64, unroll=8)
    def _(c):
        fx[pl.ds(c * PC, 64), :] = x_ref[pl.ds(pl.multiple_of(c * 64, 64), 64), :].astype(F32)

    def from_fx(r):
        parts = [fx[pl.ds(2 * r + n, 64, stride=PC), :].astype(BF) for n in range(2)]
        return jnp.concatenate(parts, axis=0)

    @pl.loop(0, 16, unroll=4)
    def _(i):
        made = mm(c0, jnp.concatenate([from_fx(2 * i), from_fx(2 * i + 1)], axis=1))
        fa[pl.ds(2 * i * PA, 128), :] = made[:, :128]
        fa[pl.ds(2 * i * PA + PA, 128), :] = made[:, 128:]

    wb0 = middle_form(real_form(g_ref, 0, 1))
    i, j = iotas(256, 256)
    perm[...] = jnp.where(j == regrouped(i), 1.0, 0.0).astype(BF)
    pl.semaphore_wait(barrier, 6 + n_lo - 1)

    def near_copy(ch, d):
        a = b0 + (1 - 2 * b0) * (d % 2)
        b = b1 + (1 - 2 * b1) * (d // 2)
        return pltpu.make_async_remote_copy(
            src_ref=s1[ch].at[b, a],
            dst_ref=y1[ch].at[b1, b0],
            send_sem=ysend.at[ch, d],
            recv_sem=yrecv.at[ch, d],
            device_id={"hi": near(d), "lo": lo},
            device_id_type=MESH,
        )

    def lo_copy(ch, j):
        to = (lo + j) % n_lo
        return pltpu.make_async_remote_copy(
            src_ref=z1[ch].at[to],
            dst_ref=r1[ch].at[lo],
            send_sem=lsend.at[ch, j],
            recv_sem=lrecv.at[ch, j],
            device_id={"hi": hi, "lo": to},
            device_id_type=MESH,
        )

    def far_copy(k, kind):
        a = b2 + (1 - 2 * b2) * (kind % 2)
        b = b3 + (1 - 2 * b3) * (kind // 2)
        src, dst, to = s2[k].at[b, a], y2[k].at[b3, b2], far(kind)
        return pltpu.make_async_remote_copy(
            src_ref=src,
            dst_ref=dst,
            send_sem=psend.at[k, kind],
            recv_sem=precv.at[k, kind],
            device_id={"hi": to, "lo": lo},
            device_id_type=MESH,
        )

    def send_near(ch):
        for d in (3, 2, 1):
            near_copy(ch, d).start()
        y1[ch][b1, b0] = s1[ch][b1, b0]

    low = lax.broadcasted_iota(jnp.int32, (32, 128), 1) < 64
    for q12 in range(2):

        @pl.loop(0, 4)
        def _(g):
            parts = []
            for k in range(4):
                for b in range(2):
                    c = b * 32 + (g * 4 + k) * 2 + q12
                    parts.append(
                        middle_operand(
                            fa[pl.ds(c, 32, stride=PA), :], fa[pl.ds(64 + c, 32, stride=PA), :]
                        )
                    )
            made = mm(wb0, jnp.concatenate(parts, axis=1))
            rows = []
            for n in range(8):
                part = made[:, 128 * n : 128 * (n + 1)]
                re = jnp.where(low, part[0:32], part[64:96]).astype(BF)
                im = jnp.where(low, part[32:64], part[96:128]).astype(BF)
                rows.append(jnp.concatenate([re, im], axis=1))
            moved = mm(jnp.concatenate(rows, axis=0), perm[...]).astype(BF)
            for n in range(8):
                for a in range(2):
                    both = moved[32 * n + 16 * a : 32 * n + 16 * a + 16]
                    s1[q12][n % 2, a, g * 4 + n // 2] = both[:, :128]
                    s1[2][n % 2, a, q12, g * 4 + n // 2] = both[:, 128:]

        send_near(q12)
    send_near(2)

    wc1[...] = half_form(after(real_form(g_ref, 3, 2), real_form(g_ref, 2, 2)))
    wb1[...] = quarter_form(after(real_form(g_ref, 2, 1), real_form(g_ref, 1, 1)))
    wb2[...] = middle_form(real_form(g_ref, 3, 1), paired=True)
    lane = after(real_form(g_ref, 1, 0), real_form(g_ref, 0, 0))
    lane2 = after(real_form(g_ref, 3, 0), real_form(g_ref, 2, 0))
    wa[...] = lane_form(after(lane2, lane))

    def pass_to_lo(ch):
        for d in range(1, 4):
            near_copy(ch, d).wait_recv()

        @pl.loop(0, n_lo, unroll=4)
        def _(to):
            t = rg_ref[to]
            for a in range(2):
                if ch < 2:
                    z1[ch][to, a] = y1[ch][t // 16, a, t % 16]
                else:
                    for q12 in range(2):
                        z1[ch][to, a, q12] = y1[ch][t // 16, a, q12, t % 16]

        @pl.loop(1, n_lo)
        def _(j):
            lo_copy(ch, j).start()

    def spread_out(ch, ref, t):
        for a in range(2):
            if ch < 2:
                fb[pl.ds((t * 2 + ch) * PB + 16 * a, 16), :] = ref[t, a].astype(F32)
            else:
                for q12 in range(2):
                    fb[pl.ds((t * 2 + q12) * PB + 16 * a, 16), :] = ref[t, a, q12].astype(F32)

    def take_from_lo(ch):
        spread_out(ch, z1[ch], lo)

        @pl.loop(1, n_lo)
        def _(j):
            lo_copy(ch, j).wait_recv()
            spread_out(ch, r1[ch], (lo + n_lo - j) % n_lo)

    def top_gate():
        left = lax.broadcasted_iota(jnp.int32, (64, 128), 1) < 64

        @pl.loop(0, 8)
        def _(g):
            parts = []
            for k in range(4):
                x = fb[pl.ds(g * 4 + k, 64, stride=PB), :]
                parts.append(
                    jnp.concatenate([x.astype(BF), pltpu.roll(x, 64, 1).astype(BF)], axis=0)
                )
            made = mm(wc1[...], jnp.concatenate(parts, axis=1))
            for k in range(4):
                part = made[:, 128 * k : 128 * (k + 1)]
                fa[pl.ds((g * 4 + k) * PC, 64), :] = jnp.where(left, part[:64], part[64:])

    quarter = lax.broadcasted_iota(jnp.int32, (32, 128), 1) // 32

    def middle_and_send(e, n_sub):
        at = e * SUB + n_sub

        @pl.loop(0, 2)
        def _(g):
            parts = []
            for k in range(4):
                for b in range(2):
                    x = fa[pl.ds(b * 32 + n_sub * 8 + g * 4 + k, 32, stride=PC), :]
                    parts.append(
                        jnp.concatenate(
                            [x.astype(BF)]
                            + [pltpu.roll(x, 128 - 32 * m, 1).astype(BF) for m in range(1, 4)],
                            axis=0,
                        )
                    )
            made = mm(wb1[...], jnp.concatenate(parts, axis=1))
            for n in range(8):
                part = made[:, 128 * n : 128 * (n + 1)]
                first = jnp.where(quarter == 0, part[0:32], part[32:64])
                second = jnp.where(quarter == 2, part[64:96], part[96:128])
                done = jnp.where(quarter < 2, first, second).astype(BF)
                for a in range(2):
                    s2[at][n % 2, a, g * 4 + n // 2] = done[16 * a : 16 * (a + 1)]

        for kind in (3, 2, 1):
            far_copy(at, kind).start()
        y2[at][b3, b2] = s2[at][b3, b2]

    for ch in range(CH):
        pass_to_lo(ch)
    take_from_lo(0)
    take_from_lo(1)
    top_gate()
    for n_sub in range(SUB):
        middle_and_send(0, n_sub)
    take_from_lo(2)
    top_gate()
    for n_sub in range(SUB):
        middle_and_send(1, n_sub)
    for ch in range(SUB):
        for e in range(2):
            for kind in range(1, 4):
                far_copy(e * SUB + ch, kind).wait_recv()

        @pl.loop(0, 2)
        def _(g):
            rows = []
            for k in range(4):
                for b in range(2):
                    for a in range(2):
                        rows.append(
                            jnp.concatenate(
                                [y2[ch][b, a, g * 4 + k], y2[SUB + ch][b, a, g * 4 + k]], axis=1
                            )
                        )
            made = mm(jnp.concatenate(rows, axis=0), wa[...])
            operand = jnp.concatenate(
                [
                    middle_operand(made[32 * n : 32 * n + 32, :128], made[32 * n : 32 * n + 32, 128:])
                    for n in range(8)
                ],
                axis=1,
            )
            whole = mm(wb2[...], operand)
            left = lax.broadcasted_iota(jnp.int32, (64, 128), 1) < 64
            for n in range(8):
                row = pl.multiple_of((n % 2 * 32 + ch * 8 + g * 4 + n // 2) * 64, 64)
                part = whole[:, 128 * n : 128 * (n + 1)]
                o_ref[pl.ds(row, 64), :] = jnp.where(left, part[:64], part[64:]).astype(BF)

    for ch in range(CH):
        for d in range(1, 4):
            near_copy(ch, d).wait_send()

        @pl.loop(1, n_lo)
        def _(j):
            lo_copy(ch, j).wait_send()

    for at in range(2 * SUB):
        for kind in range(1, 4):
            far_copy(at, kind).wait_send()


def on_device(state, gates, regroup):
    n_lo = lax.axis_size("lo")
    vmem = pl.BlockSpec(memory_space=pltpu.VMEM)
    x = state.reshape(2, 2048, 128).transpose(1, 0, 2).reshape(4096, 128)
    quarter = (2, 2, 16, 16, 128)
    by_lo = (n_lo, 2, 16, 128)
    scratch = (
        [pltpu.VMEM(quarter, BF)] * 2
        + [pltpu.VMEM((2, 2, 2, 16, 16, 128), BF)]
        + [pltpu.VMEM(quarter, BF)] * 2
        + [pltpu.VMEM((2, 2, 2, 16, 16, 128), BF)]
        + [pltpu.VMEM(by_lo, BF)] * 2
        + [pltpu.VMEM((n_lo, 2, 2, 16, 128), BF)]
        + [pltpu.VMEM(by_lo, BF)] * 2
        + [pltpu.VMEM((n_lo, 2, 2, 16, 128), BF)]
        + [pltpu.VMEM((2, 2, 8, 16, 128), BF)] * 16
        + [pltpu.VMEM((32 * PA, 128), F32), pltpu.VMEM((64 * PB, 128), F32), pltpu.VMEM((64 * PC, 128), F32)]
        + [pltpu.VMEM((128, 128), BF)] * 3
        + [pltpu.VMEM((256, 256), BF)] * 2
        + [pltpu.SemaphoreType.DMA((CH, 4))] * 2
        + [pltpu.SemaphoreType.DMA((CH, n_lo))] * 2
        + [pltpu.SemaphoreType.DMA((2 * SUB, 4))] * 2
    )
    out = pl.pallas_call(
        functools.partial(kernel, n_lo),
        out_shape=jax.ShapeDtypeStruct((4096, 128), BF),
        in_specs=[vmem, vmem, pl.BlockSpec(memory_space=pltpu.SMEM)],
        out_specs=vmem,
        scratch_shapes=scratch,
        compiler_params=pltpu.CompilerParams(
            collective_id=0, has_side_effects=True, vmem_limit_bytes=40 * 1024 * 1024
        ),
        name="circuit",
    )(x, gates, regroup)
    return out.reshape(2048, 2, 128).transpose(1, 0, 2).reshape(2, -1)


def solution(mesh):
    placed = (P(None, ("hi", "lo")), P(), P())
    return jax.shard_map(
        on_device, mesh=mesh, in_specs=placed, out_specs=P(None, ("hi", "lo")), check_vma=False
    )
```

```python
import functools

import jax
import jax.numpy as jnp
from jax import lax
from jax.experimental import pallas as pl
from jax.experimental.pallas import tpu as pltpu
from jax.sharding import PartitionSpec as P

BF = jnp.bfloat16
F32 = jnp.float32
MESH = pl.DeviceIdType.MESH
CH = 5
PIECES = ((0, 0, 8), (0, 8, 8), (1, 0, 16), (0, 0, 16), (1, 0, 16))
SUB = 4
PA = 129
PB = 33
PC = 65


def mm(a, b):
    return lax.dot_general(a, b, (((1,), (0,)), ((), ())), preferred_element_type=F32)


def mm_t(a, b):
    return lax.dot_general(a, b, (((1,), (1,)), ((), ())), preferred_element_type=F32)


def real_form(g_ref, layer, j):
    re = g_ref[layer, j, 0]
    im = g_ref[layer, j, 1]
    upper = jnp.concatenate([re, -im], axis=1)
    lower = jnp.concatenate([im, re], axis=1)
    return jnp.concatenate([upper, lower], axis=0)


def after(second, first):
    return mm(second, first).astype(BF)


def iotas(rows, cols):
    return (
        lax.broadcasted_iota(jnp.int32, (rows, cols), 0),
        lax.broadcasted_iota(jnp.int32, (rows, cols), 1),
    )


def middle_form(whole, paired=False):
    i, j = iotas(128, 128)
    pick = jnp.where(j == (i // 32 % 2) * 64 + (i % 32) * 2 + i // 64, 1.0, 0.0).astype(BF)
    order = pick
    if paired:
        order = jnp.where(j == (i % 2) * 64 + i // 2 % 32 * 2 + i // 64, 1.0, 0.0).astype(BF)
    both = mm_t(mm(order, whole).astype(BF), pick)
    return jnp.concatenate([both[:64], pltpu.roll(both[64:], 64, 1)], axis=0).astype(BF)


def quarter_form(whole):
    i, j = iotas(128, 128)
    pick = jnp.where(j == (i // 64) * 64 + (i % 32) * 2 + i // 32 % 2, 1.0, 0.0).astype(BF)
    both = mm_t(mm(pick, whole).astype(BF), pick)
    rows = [both[:32]]
    for n in range(1, 4):
        rows.append(pltpu.roll(both[32 * n : 32 * n + 32], 128 - 32 * n, 1))
    return jnp.concatenate(rows, axis=0).astype(BF)


def half_form(whole):
    lower = pltpu.roll(whole[64:].astype(F32), 64, 1)
    return jnp.concatenate([whole[:64], lower.astype(BF)], axis=0)


def regrouped(i):
    return (i // 32 % 2) * 128 + (i // 128) * 64 + (i // 64 % 2) * 32 + i % 32


def lane_form(whole):
    i, j = iotas(256, 128)
    spread = jnp.where(j == (i // 128) * 64 + i % 64, 1.0, 0.0).astype(BF)
    wide = mm_t(mm_t(spread, whole).astype(BF), spread)
    i, j = iotas(256, 256)
    natural = jnp.where(i // 64 % 2 == j // 64 % 2, wide, 0.0).astype(BF)
    back = jnp.where(i == regrouped(j), 1.0, 0.0).astype(BF)
    return mm(back, natural).astype(BF)


def middle_operand(re, im):
    return jnp.concatenate(
        [re.astype(BF), im.astype(BF), pltpu.roll(re, 64, 1).astype(BF), pltpu.roll(im, 64, 1).astype(BF)],
        axis=0,
    )


def kernel(n_lo, x_ref, g_ref, rg_ref, o_ref, *scratch):
    s1 = scratch[0:5]
    y1 = scratch[5:10]
    z1 = scratch[10:15]
    r1 = scratch[15:20]
    s2 = scratch[20:28]
    y2 = scratch[28:36]
    fa, fb, wc1, wb1, wb2, wa, perm = scratch[36:43]
    ysend, yrecv, lsend, lrecv, psend, precv = scratch[43:49]
    hi = lax.axis_index("hi")
    lo = lax.axis_index("lo")
    b0, b1, b2, b3 = hi % 2, hi // 2 % 2, hi // 4 % 2, hi // 8 % 2

    def near(d):
        return hi + (1 - 2 * b0) * (d % 2) + 2 * (1 - 2 * b1) * (d // 2)

    def far(d):
        return hi + 4 * (1 - 2 * b2) * (d % 2) + 8 * (1 - 2 * b3) * (d // 2)

    barrier = pltpu.get_barrier_semaphore()
    for to in (near(1), near(2), near(3), far(1), far(2), far(3)):
        pl.semaphore_signal(barrier, inc=1, device_id={"hi": to, "lo": lo}, device_id_type=MESH)

    @pl.loop(1, n_lo)
    def _(j):
        pl.semaphore_signal(
            barrier, inc=1, device_id={"hi": hi, "lo": (lo + j) % n_lo}, device_id_type=MESH
        )

    c0 = after(real_form(g_ref, 1, 2), real_form(g_ref, 0, 2))

    @pl.loop(0, 16, unroll=4)
    def _(i):
        made = mm(c0, x_ref[:, pl.ds(pl.multiple_of(i * 256, 256), 256)])
        fa[pl.ds(2 * i * PA, 128), :] = made[:, :128]
        fa[pl.ds(2 * i * PA + PA, 128), :] = made[:, 128:]

    wb0 = middle_form(real_form(g_ref, 0, 1))
    i, j = iotas(256, 256)
    perm[...] = jnp.where(j == regrouped(i), 1.0, 0.0).astype(BF)
    pl.semaphore_wait(barrier, 6 + n_lo - 1)

    def near_copy(ch, d):
        a = b0 + (1 - 2 * b0) * (d % 2)
        b = b1 + (1 - 2 * b1) * (d // 2)
        return pltpu.make_async_remote_copy(
            src_ref=s1[ch].at[b, a],
            dst_ref=y1[ch].at[b1, b0],
            send_sem=ysend.at[ch, d],
            recv_sem=yrecv.at[ch, d],
            device_id={"hi": near(d), "lo": lo},
            device_id_type=MESH,
        )

    def lo_copy(ch, j):
        to = (lo + j) % n_lo
        return pltpu.make_async_remote_copy(
            src_ref=z1[ch].at[to],
            dst_ref=r1[ch].at[lo],
            send_sem=lsend.at[ch, j],
            recv_sem=lrecv.at[ch, j],
            device_id={"hi": hi, "lo": to},
            device_id_type=MESH,
        )

    def far_copy(k, kind):
        a = b2 + (1 - 2 * b2) * (kind % 2)
        b = b3 + (1 - 2 * b3) * (kind // 2)
        src, dst, to = s2[k].at[b, a], y2[k].at[b3, b2], far(kind)
        return pltpu.make_async_remote_copy(
            src_ref=src,
            dst_ref=dst,
            send_sem=psend.at[k, kind],
            recv_sem=precv.at[k, kind],
            device_id={"hi": to, "lo": lo},
            device_id_type=MESH,
        )

    def send_near(ch):
        for d in (3, 2, 1):
            near_copy(ch, d).start()
        y1[ch][b1, b0] = s1[ch][b1, b0]

    low = lax.broadcasted_iota(jnp.int32, (32, 128), 1) < 64
    for q12 in range(2):

        @pl.loop(0, 4)
        def _(g):
            parts = []
            for k in range(4):
                for b in range(2):
                    c = b * 32 + (g * 4 + k) * 2 + q12
                    parts.append(
                        middle_operand(
                            fa[pl.ds(c, 32, stride=PA), :], fa[pl.ds(64 + c, 32, stride=PA), :]
                        )
                    )
            made = mm(wb0, jnp.concatenate(parts, axis=1))
            rows = []
            for n in range(8):
                part = made[:, 128 * n : 128 * (n + 1)]
                re = jnp.where(low, part[0:32], part[64:96]).astype(BF)
                im = jnp.where(low, part[32:64], part[96:128]).astype(BF)
                rows.append(jnp.concatenate([re, im], axis=1))
            moved = mm(jnp.concatenate(rows, axis=0), perm[...]).astype(BF)
            for n in range(8):
                for e in range(2):
                    for a in range(2):
                        tile = moved[32 * n + 16 * a : 32 * n + 16 * a + 16, 128 * e : 128 * (e + 1)]
                        if e == 0 and q12 == 0:
                            s1[0][n % 2, a, g * 4 + n // 2] = tile[:8]
                            s1[1][n % 2, a, g * 4 + n // 2] = tile[8:]
                        else:
                            s1[e * 2 + q12 + 1][n % 2, a, g * 4 + n // 2] = tile

        if q12 == 0:
            send_near(0)
        send_near(q12 + 1)
    send_near(3)
    send_near(4)

    wc1[...] = half_form(after(real_form(g_ref, 3, 2), real_form(g_ref, 2, 2)))
    wb1[...] = quarter_form(after(real_form(g_ref, 2, 1), real_form(g_ref, 1, 1)))
    wb2[...] = middle_form(real_form(g_ref, 3, 1), paired=True)
    lane = after(real_form(g_ref, 1, 0), real_form(g_ref, 0, 0))
    lane2 = after(real_form(g_ref, 3, 0), real_form(g_ref, 2, 0))
    wa[...] = lane_form(after(lane2, lane))

    def pass_to_lo(ch):
        for d in range(1, 4):
            near_copy(ch, d).wait_recv()

        @pl.loop(0, n_lo, unroll=4)
        def _(to):
            t = rg_ref[to]
            z1[ch][to, 0] = y1[ch][t // 16, 0, t % 16]
            z1[ch][to, 1] = y1[ch][t // 16, 1, t % 16]

        @pl.loop(1, n_lo)
        def _(j):
            lo_copy(ch, j).start()

    def spread_out(ch, ref, t):
        for a in range(2):
            q12, first, rows = PIECES[ch]
            fb[pl.ds((t * 2 + q12) * PB + 16 * a + first, rows), :] = ref[t, a].astype(F32)

    def take_from_lo(ch):
        spread_out(ch, z1[ch], lo)

        @pl.loop(1, n_lo)
        def _(j):
            lo_copy(ch, j).wait_recv()

        @pl.loop(1, n_lo)
        def _(j):
            spread_out(ch, r1[ch], (lo + j) % n_lo)

    def top_gate():
        left = lax.broadcasted_iota(jnp.int32, (64, 128), 1) < 64

        @pl.loop(0, 8)
        def _(g):
            parts = []
            for k in range(4):
                x = fb[pl.ds(g * 4 + k, 64, stride=PB), :]
                parts.append(
                    jnp.concatenate([x.astype(BF), pltpu.roll(x, 64, 1).astype(BF)], axis=0)
                )
            made = mm(wc1[...], jnp.concatenate(parts, axis=1))
            for k in range(4):
                part = made[:, 128 * k : 128 * (k + 1)]
                fa[pl.ds((g * 4 + k) * PC, 64), :] = jnp.where(left, part[:64], part[64:])

    quarter = lax.broadcasted_iota(jnp.int32, (32, 128), 1) // 32

    def middle_and_send(e, n_sub):
        at = e * SUB + n_sub

        @pl.loop(0, 2)
        def _(g):
            parts = []
            for k in range(4):
                for b in range(2):
                    x = fa[pl.ds(b * 32 + n_sub * 8 + g * 4 + k, 32, stride=PC), :]
                    parts.append(
                        jnp.concatenate(
                            [x.astype(BF)]
                            + [pltpu.roll(x, 128 - 32 * m, 1).astype(BF) for m in range(1, 4)],
                            axis=0,
                        )
                    )
            made = mm(wb1[...], jnp.concatenate(parts, axis=1))
            for n in range(8):
                part = made[:, 128 * n : 128 * (n + 1)]
                first = jnp.where(quarter == 0, part[0:32], part[32:64])
                second = jnp.where(quarter == 2, part[64:96], part[96:128])
                done = jnp.where(quarter < 2, first, second).astype(BF)
                for a in range(2):
                    s2[at][n % 2, a, g * 4 + n // 2] = done[16 * a : 16 * (a + 1)]

        for kind in (3, 2, 1):
            far_copy(at, kind).start()
        y2[at][b3, b2] = s2[at][b3, b2]

    for ch in range(CH):
        pass_to_lo(ch)
    take_from_lo(0)
    take_from_lo(1)
    take_from_lo(2)
    top_gate()
    for n_sub in range(SUB):
        middle_and_send(0, n_sub)
    take_from_lo(3)
    take_from_lo(4)
    top_gate()
    for n_sub in range(SUB):
        middle_and_send(1, n_sub)
    for ch in range(SUB):
        for e in range(2):
            for kind in range(1, 4):
                far_copy(e * SUB + ch, kind).wait_recv()

        @pl.loop(0, 2)
        def _(g):
            rows = []
            for k in range(4):
                for b in range(2):
                    for a in range(2):
                        rows.append(
                            jnp.concatenate(
                                [y2[ch][b, a, g * 4 + k], y2[SUB + ch][b, a, g * 4 + k]], axis=1
                            )
                        )
            made = mm(jnp.concatenate(rows, axis=0), wa[...])
            operand = jnp.concatenate(
                [
                    middle_operand(made[32 * n : 32 * n + 32, :128], made[32 * n : 32 * n + 32, 128:])
                    for n in range(8)
                ],
                axis=1,
            )
            whole = mm(wb2[...], operand)
            left = lax.broadcasted_iota(jnp.int32, (64, 128), 1) < 64
            for n in range(8):
                row = pl.multiple_of((n % 2 * 32 + ch * 8 + g * 4 + n // 2) * 64, 64)
                part = whole[:, 128 * n : 128 * (n + 1)]
                o_ref[pl.ds(row, 64), :] = jnp.where(left, part[:64], part[64:]).astype(BF)

    for ch in range(CH):
        for d in range(1, 4):
            near_copy(ch, d).wait_send()

        @pl.loop(1, n_lo)
        def _(j):
            lo_copy(ch, j).wait_send()

    for at in range(2 * SUB):
        for kind in range(1, 4):
            far_copy(at, kind).wait_send()


def on_device(state, gates, regroup):
    n_lo = lax.axis_size("lo")
    vmem = pl.BlockSpec(memory_space=pltpu.VMEM)
    x = state.reshape(128, 4096)
    scratch = (
        [pltpu.VMEM((2, 2, 16, rows, 128), BF) for _, _, rows in PIECES] * 2
        + [pltpu.VMEM((n_lo, 2, rows, 128), BF) for _, _, rows in PIECES] * 2
        + [pltpu.VMEM((2, 2, 8, 16, 128), BF)] * 16
        + [pltpu.VMEM((32 * PA, 128), F32), pltpu.VMEM((64 * PB, 128), F32)]
        + [pltpu.VMEM((128, 128), BF)] * 3
        + [pltpu.VMEM((256, 256), BF)] * 2
        + [pltpu.SemaphoreType.DMA((CH, 4))] * 2
        + [pltpu.SemaphoreType.DMA((CH, n_lo))] * 2
        + [pltpu.SemaphoreType.DMA((2 * SUB, 4))] * 2
    )
    out = pl.pallas_call(
        functools.partial(kernel, n_lo),
        out_shape=jax.ShapeDtypeStruct((4096, 128), BF),
        in_specs=[vmem, vmem, pl.BlockSpec(memory_space=pltpu.SMEM)],
        out_specs=vmem,
        scratch_shapes=scratch,
        compiler_params=pltpu.CompilerParams(
            collective_id=0, has_side_effects=True, vmem_limit_bytes=40 * 1024 * 1024
        ),
        name="circuit",
    )(x, gates, regroup)
    return out.reshape(2048, 2, 128).transpose(1, 0, 2).reshape(2, -1)


def solution(mesh):
    placed = (P(None, ("hi", "lo")), P(), P())
    return jax.shard_map(
        on_device, mesh=mesh, in_specs=placed, out_specs=P(None, ("hi", "lo")), check_vma=False
    )
```
